32 devices in a mesh: dom: 8 (over z, x), rep: 4 (over y, core).
Axes of the slice: x: 2, y: 2, z: 4, core: 2. Of those that a mesh axis runs over, the one named last changes fastest.
Arguments:
- features: bfloat16 [65536, 128], P('dom'), may hold values from -6 to 6
- weight: bfloat16 [128, 256], replicated, may hold values from -0.5 to 0.5
- out_grad: bfloat16 [65536, 256], P(('dom', 'rep')), may hold values from -6 to 6
- send_rows: int32 [8, 8, 64], P('dom'), may hold values from 0 to 8191, as said below
- send_count: int32 [8, 8], P('dom'), may hold values from 0 to 64, as said below
- tile_target: int32 [8, 4, 256], P('dom', 'rep'), may hold values from 0 to 15, as said below
- tile_source: int32 [8, 4, 256], P('dom', 'rep'), may hold values from 0 to 67, as said below
- tile_weights: bfloat16 [8, 4, 256, 128, 128], P('dom', 'rep'), may hold values from -0.125 to 0.125
Outputs:
- activated: bfloat16 [65536, 256], P(('dom', 'rep'))
- feature_grad: bfloat16 [65536, 128], P(('dom', 'rep'))
- weight_grad: float32 [128, 256], replicated
The draws below stay inside these ranges and needn't reach their ends.
Inputs may be any that keep to these rules, and one draw needn't show every extreme that they name: Within one list send_rows[o, d] the rows are distinct and increasing; entries at slots c >= send_count[o, d] are ignored. send_count[o, o] is 0. Every owner sends exactly 64 rows to some partition, and every partition receives exactly 64 rows from some owner. `tile_target`: pairs of target and source tiles may repeat. `tile_source`: every halo source tile (64 to 67) is named by some tile of every group.
All inputs are finite; a program needn't handle non-finite values.
Results may differ from the reference program's by a relative error of at most 0.006.
Values may be sent and summed in bfloat16 or wider, within the bound.
No kernel may reach another device: no remote copies, remote signals or barrier semaphores. Data moves between devices by JAX's collectives and lax.ppermute only.
A program may use at most 128 MiB of HBM per device.

```python
import jax
import jax.numpy as jnp
from jax import lax

FEAT = 128
HIDDEN_SIZE = 256
TILE = 128
TILES_PER = 16
CAP = 64
TGT_DEV = 2048
NODES_DEV = 8192
NODES = 65536
TGT_TILES = 16
LOCAL_TILES = 64
HALO_TILES = 4
SRC_TILES = 68
NTILE = 256
N_DOM = 8
N_REP = 4


def draw_send_count(key, part):
    first, second, third = jax.random.split(jax.random.fold_in(key, 11), 3)
    one = jax.random.randint(first, (N_DOM, N_DOM), 0, CAP + 1)
    two = jax.random.randint(second, (N_DOM, N_DOM), 0, CAP + 1)
    counts = jnp.maximum(one, two)
    offset = jax.random.randint(third, (), 1, N_DOM)
    owners = jnp.arange(N_DOM)[:, None]
    dests = jnp.arange(N_DOM)[None, :]
    counts = jnp.where((owners + offset) % N_DOM == dests, CAP, counts)
    counts = jnp.where(owners == dests, 0, counts)
    return counts.astype(jnp.int32)


def draw_send_rows(key, part):
    first, second = jax.random.split(jax.random.fold_in(key, 23), 2)
    stride = jax.random.randint(first, (N_DOM, N_DOM, 1), 1, NODES_DEV // CAP)
    base = jax.random.randint(second, (N_DOM, N_DOM, 1), 0, NODES_DEV - (CAP - 1) * stride)
    rows = base + jnp.arange(CAP)[None, None, :] * stride
    return rows.astype(jnp.int32)


def draw_tile_target(key, part):
    picked = jax.random.randint(jax.random.fold_in(key, 37), (N_DOM, N_REP, NTILE), 0, TGT_TILES)
    return picked.astype(jnp.int32)


def draw_tile_source(key, part):
    picked = jax.random.randint(jax.random.fold_in(key, 41), (N_DOM, N_REP, NTILE), 0, SRC_TILES)
    place = jnp.arange(NTILE)[None, None, :]
    picked = jnp.where(place < HALO_TILES, LOCAL_TILES + place, picked)
    return picked.astype(jnp.int32)


def block_levels(key, extent, cuts, low, largest):
    level = 1.0
    for dim, blocks in cuts:
        heights = jax.random.uniform(jax.random.fold_in(jax.random.fold_in(key, 6), dim), (blocks,), jnp.float32, low / len(cuts), largest / len(cuts))
        level = level * jnp.repeat(jnp.exp(heights), extent[dim] // blocks).reshape((-1,) + (1,) * (len(extent) - 1 - dim))
    return level


def noise(stream_key, shape, deviation, bound, pieces=(), held_as=jnp.bfloat16):
    loudness = block_levels(stream_key, shape, pieces, -0.22, 0.18) if pieces else 1.0
    entries = jax.random.normal(stream_key, shape, jnp.float32) * deviation * loudness
    return jnp.minimum(jnp.maximum(entries, -bound), bound).astype(held_as)


def setup_inputs(seed: int = 0) -> dict:
    key_list = jax.random.split(jax.random.key(seed), 9)
    features = noise(key_list[0], (NODES, FEAT), 1.0, 6.0, ((0, 8),))
    weight = noise(key_list[1], (FEAT, HIDDEN_SIZE), FEAT ** -0.5, 0.5)
    out_grad = noise(key_list[2], (NODES, HIDDEN_SIZE), 1.0, 6.0, ((0, 32),))
    send_rows = draw_send_rows(jax.random.fold_in(key_list[8], 71), 0)
    send_count = draw_send_count(jax.random.fold_in(key_list[8], 71), 0)
    tile_target = draw_tile_target(jax.random.fold_in(key_list[8], 71), 0)
    tile_source = draw_tile_source(jax.random.fold_in(key_list[8], 71), 0)
    tile_weights = noise(key_list[7], (N_DOM, N_REP, NTILE, TILE, TILE), (TILES_PER * TILE) ** -0.5, 0.125, ((0, 8), (1, 4)))
    return dict(features=features, weight=weight, out_grad=out_grad, send_rows=send_rows, send_count=send_count, tile_target=tile_target, tile_source=tile_source, tile_weights=tile_weights)


def device_pass(sources, weights_tiles, targets, anchors, grad_rows, weight):
    tile = weights_tiles.shape[-1]
    feat = sources.shape[1]
    blocks = sources.reshape(-1, tile, feat)[anchors]
    prods = jnp.einsum("tij,tjf->tif", weights_tiles.astype(jnp.float32), blocks.astype(jnp.float32), precision=lax.Precision.HIGHEST)
    gathered = jax.ops.segment_sum(prods, targets, num_segments=TGT_TILES).reshape(TGT_DEV, feat).astype(jnp.bfloat16)
    pre = jnp.dot(gathered, weight, preferred_element_type=jnp.float32)
    activated = jax.nn.silu(pre).astype(jnp.bfloat16)
    sigma = jax.nn.sigmoid(pre)
    slope = sigma * (1.0 + pre * (1.0 - sigma))
    pre_grad = (grad_rows.astype(jnp.float32) * slope).astype(jnp.bfloat16)
    weight_part = jnp.dot(gathered.T, pre_grad, preferred_element_type=jnp.float32)
    agg_grad = jnp.dot(pre_grad, weight.T, preferred_element_type=jnp.float32).astype(jnp.bfloat16)
    dblocks = agg_grad.reshape(TGT_TILES, tile, feat)[targets]
    backward = jnp.einsum("tij,tif->tjf", weights_tiles.astype(jnp.float32), dblocks.astype(jnp.float32), precision=lax.Precision.HIGHEST)
    source_grad = jax.ops.segment_sum(backward, anchors, num_segments=SRC_TILES).reshape(-1, feat)
    return activated, weight_part, source_grad


def reference(features, weight, out_grad, send_rows, send_count, tile_target, tile_source, tile_weights):
    owned = features.reshape(N_DOM, NODES_DEV, FEAT)
    slots = jnp.arange(CAP, dtype=jnp.int32)
    valid = slots[None, None, :] < send_count[:, :, None]
    sent = jax.vmap(lambda block, index: block[index])(owned, send_rows)
    sent = jnp.where(valid[..., None], sent, jnp.zeros((), jnp.bfloat16))
    halo = jnp.transpose(sent, (1, 0, 2, 3)).reshape(N_DOM, N_DOM * CAP, FEAT)
    grads = out_grad.reshape(N_DOM, N_REP, TGT_DEV, HIDDEN_SIZE)

    def one_part(carry, part):
        sources = jnp.concatenate([owned[part], halo[part]], axis=0)
        outputs = []
        total = jnp.zeros((SRC_TILES * TILE, FEAT), jnp.float32)
        for rank in range(N_REP):
            act, part_w, part_s = device_pass(sources, tile_weights[part, rank], tile_target[part, rank], tile_source[part, rank], grads[part, rank], weight)
            outputs.append(act)
            carry = carry + part_w
            total = total + part_s
        return carry, (jnp.stack(outputs), total)

    weight_grad, (acts, totals) = lax.scan(one_part, jnp.zeros((FEAT, HIDDEN_SIZE), jnp.float32), jnp.arange(N_DOM, dtype=jnp.int32))
    local = totals[:, :NODES_DEV]
    returned = totals[:, NODES_DEV:].reshape(N_DOM, N_DOM, CAP, FEAT)
    returned = jnp.transpose(returned, (1, 0, 2, 3))
    returned = jnp.where(valid[..., None], returned, jnp.zeros((), jnp.float32))
    local = jax.vmap(lambda acc, index, rows: acc.at[index.reshape(-1)].add(rows.reshape(-1, FEAT)))(local, send_rows, returned)
    return acts.reshape(NODES, HIDDEN_SIZE), local.reshape(NODES, FEAT).astype(jnp.bfloat16), weight_grad
```

```python
import functools

import jax
import jax.numpy as jnp
from jax import lax
from jax.experimental import pallas as pl
from jax.experimental.pallas import tpu as pltpu
from jax.sharding import PartitionSpec as P

GROUP = 8
F32 = jnp.float32
BF16 = jnp.bfloat16
MIB = 1 << 20
VMEM = pl.BlockSpec(memory_space=pltpu.VMEM)
SMEM = pl.BlockSpec(memory_space=pltpu.SMEM)
ANY = pl.BlockSpec(memory_space=pl.ANY)
NN = (((1,), (0,)), ((), ()))
NT = (((1,), (1,)), ((), ()))
TN = (((0,), (0,)), ((), ()))


def dot(a, b, dims=NN):
    return lax.dot_general(a, b, dims, preferred_element_type=F32)


def block(i, size):
    return pl.ds(pl.multiple_of(i * size, size), size)


def pick_kernel(rows, counts, feat, out, wide, stage):
    dests, cap = rows.shape
    step = 512

    def widen(i, carry):
        wide[block(i, step), :] = feat[block(i, step), :].astype(F32)
        return carry

    lax.fori_loop(0, feat.shape[0] // step, widen, 0)
    slot = lax.broadcasted_iota(jnp.int32, stage.shape, 0)

    def one(d, carry):
        count = counts[0, d]
        for c in range(cap):
            row = jnp.where(c < count, rows[d, c], 0)
            stage[c : c + 1, :] = wide[pl.ds(row, 1), :]
        out[block(d, cap), :] = jnp.where(slot < count, stage[...], 0.0).astype(BF16)
        return carry

    lax.fori_loop(0, dests, one, 0)


def pick(rows, counts, features):
    dests, cap = rows.shape
    feat = features.shape[1]
    return pl.pallas_call(
        pick_kernel,
        name="pick",
        out_shape=jax.ShapeDtypeStruct((dests * cap, feat), BF16),
        in_specs=[SMEM, SMEM, VMEM],
        out_specs=VMEM,
        scratch_shapes=[pltpu.VMEM(features.shape, F32), pltpu.VMEM((cap, feat), F32)],
        compiler_params=pltpu.CompilerParams(vmem_limit_bytes=16 * MIB),
        cost_estimate=pl.CostEstimate(
            flops=features.size, bytes_accessed=features.size * 2, transcendentals=0
        ),
    )(rows, counts, features)


def plan_kernel(local, halo, quarter, ranks, source, target, out):
    count = source.shape[1]
    me = lax.axis_index("rep")
    src = source[...]
    part = jnp.zeros_like(src)
    for k in range(1, ranks):
        part = part + jnp.where(src >= k * quarter, 1, 0)
    place = (part ^ (me ^ (ranks - 1))) * quarter + (src - part * quarter)
    key = jnp.where(src < local, halo + place, src - local).astype(F32)
    lanes = jnp.broadcast_to(key, (count, count))
    subs = lanes.T
    i = lax.broadcasted_iota(jnp.int32, (count, count), 0)
    j = lax.broadcasted_iota(jnp.int32, (count, count), 1)
    ahead = (lanes < subs) | ((lanes == subs) & (j < i))
    spot = jnp.sum(jnp.where(ahead, 1.0, 0.0), axis=1, keepdims=True).astype(jnp.int32)
    chosen = spot == j
    tgt = jnp.broadcast_to(target[...].astype(F32), (count, count)).T

    def ordered(values):
        return jnp.sum(jnp.where(chosen, values, 0.0), axis=0, keepdims=True)

    lane = lax.broadcasted_iota(jnp.int32, (1, count), 1)
    bounds = jnp.zeros((1, count), F32)
    for b in range(ranks + 1):
        below = jnp.sum(jnp.where(key < halo + b * quarter, 1.0, 0.0), axis=1, keepdims=True)
        bounds = bounds + jnp.where(lane == b, below, 0.0)
    rest = jnp.zeros((4, count), F32)
    table = [ordered(i.astype(F32)), ordered(tgt), ordered(subs), bounds, rest]
    out[...] = jnp.concatenate(table, axis=0).astype(jnp.int32)


def plan(source, target, local, halo, ranks):
    count = source.shape[1]
    return pl.pallas_call(
        functools.partial(plan_kernel, local, halo, local // ranks, ranks),
        name="plan",
        out_shape=jax.ShapeDtypeStruct((8, count), jnp.int32),
        in_specs=[VMEM, VMEM],
        out_specs=VMEM,
        compiler_params=pltpu.CompilerParams(vmem_limit_bytes=16 * MIB),
        cost_estimate=pl.CostEstimate(
            flops=8 * count * count, bytes_accessed=16 * count, transcendentals=0
        ),
    )(source, target)


def forward_kernel(source, target, feat, tiles, acc, held, sems):
    count, tile, _ = tiles.shape
    groups = count // GROUP
    local = feat.shape[0] // tile
    spare = acc.shape[0] - 1

    def fetch(g):
        span = block(g, GROUP)
        return pltpu.make_async_copy(tiles.at[span], held.at[span], sems.at[g])

    def start(g, carry):
        fetch(g).start()
        return carry

    lax.fori_loop(0, groups, start, 0)

    def clear(k, carry):
        acc[k] = jnp.zeros(acc.shape[1:], F32)
        return carry

    lax.fori_loop(0, spare + 1, clear, 0)

    def run(g, carry):
        fetch(g).wait()
        prods = []
        for u in range(GROUP):
            s = jnp.minimum(source[0, g * GROUP + u], local - 1)
            prods.append(dot(held[g * GROUP + u], feat[block(s, tile), :]))
        for u in range(GROUP):
            t = g * GROUP + u
            k = jnp.where(source[0, t] < local, target[0, t], spare)
            acc[k] += prods[u]
        return carry

    lax.fori_loop(0, groups, run, 0)


def forward(source, target, features, tiles, targets):
    count, tile, _ = tiles.shape
    feat = features.shape[1]
    return pl.pallas_call(
        forward_kernel,
        name="forward",
        out_shape=jax.ShapeDtypeStruct((targets + 1, tile, feat), F32),
        in_specs=[SMEM, SMEM, VMEM, ANY],
        out_specs=VMEM,
        scratch_shapes=[
            pltpu.VMEM(tiles.shape, BF16),
            pltpu.SemaphoreType.DMA((count // GROUP,)),
        ],
        compiler_params=pltpu.CompilerParams(vmem_limit_bytes=24 * MIB),
        cost_estimate=pl.CostEstimate(
            flops=2 * tiles.size * feat * 4, bytes_accessed=tiles.size * 2, transcendentals=0
        ),
    )(source, target, features, tiles)


def groups_of(low, high):
    return lax.div(high - low + GROUP - 1, GROUP)


def start_run(table, tiles, held, sems, low, high):
    def start(g, carry):
        for u in range(GROUP):
            t = table[0, jnp.minimum(low + g * GROUP + u, high - 1)]
            pltpu.make_async_copy(tiles.at[t], held.at[g * GROUP + u], sems.at[g]).start()
        return carry

    lax.fori_loop(0, groups_of(low, high), start, 0)


def wait_group(tiles, held, sems, g):
    pltpu.make_async_copy(
        tiles.at[pl.ds(0, GROUP)], held.at[block(g, GROUP)], sems.at[g]
    ).wait()


def backward_run(table, grads, tiles, held, sems, acc, low, high, first):
    spare = acc.shape[0] - 1

    def run(g, carry):
        wait_group(tiles, held, sems, g)
        prods, places = [], []
        for u in range(GROUP):
            spot = low + g * GROUP + u
            at = jnp.minimum(spot, high - 1)
            prods.append(dot(grads[table[1, at]], held[g * GROUP + u]))
            places.append(jnp.where(spot < high, table[2, at] - first, spare))
        for u in range(GROUP):
            acc[places[u]] += prods[u]
        return carry

    lax.fori_loop(0, groups_of(low, high), run, 0)


def clear_tiles(acc):
    def clear(k, carry):
        acc[k] = jnp.zeros(acc.shape[1:], acc.dtype)
        return carry

    lax.fori_loop(0, acc.shape[0], clear, 0)


def middle_kernel(
    table, acc, halo, weight, out_grad, tiles, act, grads, wgrad, back, held, sums, hsum, sems
):
    _, tile, feat = acc.shape
    targets = acc.shape[0] - 1
    high = table[3, 0]
    halos = halo.shape[0] // tile
    start_run(table, tiles, held, sems, 0, high)
    clear_tiles(sums)
    clear_tiles(hsum)

    def add(g, carry):
        wait_group(tiles, held, sems, g)
        prods, places = [], []
        for u in range(GROUP):
            spot = g * GROUP + u
            at = jnp.minimum(spot, high - 1)
            prods.append(dot(held[spot], halo[block(table[2, at], tile), :]))
            places.append(jnp.where(spot < high, table[1, at], targets))
        for u in range(GROUP):
            sums[places[u]] += prods[u]
        return carry

    lax.fori_loop(0, groups_of(0, high), add, 0)
    wgrad[...] = jnp.zeros(wgrad.shape, F32)
    width = 2

    def dense(b, carry):
        many = []
        for u in range(width):
            k = b * width + u
            many.append((acc[k] + sums[k]).astype(BF16))
        rows = jnp.concatenate(many, axis=0)
        span = block(b, width * tile)
        pre = dot(rows, weight[...])
        sigma = jax.nn.sigmoid(pre)
        act[span, :] = (pre * sigma).astype(BF16)
        slope = sigma * (1.0 + pre * (1.0 - sigma))
        pre_grad = (out_grad[span, :].astype(F32) * slope).astype(BF16)
        wgrad[...] += dot(rows, pre_grad, TN)
        turned = dot(weight[...], pre_grad, NT).astype(BF16)
        for u in range(width):
            grads[b * width + u] = turned[:, u * tile : (u + 1) * tile]
        return carry

    lax.fori_loop(0, targets // width, dense, 0)

    def back_run(g, carry):
        prods, places = [], []
        for u in range(GROUP):
            spot = g * GROUP + u
            at = jnp.minimum(spot, high - 1)
            prods.append(dot(grads[table[1, at]], held[spot]))
            places.append(jnp.where(spot < high, table[2, at], halos))
        for u in range(GROUP):
            hsum[places[u]] += prods[u]
        return carry

    lax.fori_loop(0, groups_of(0, high), back_run, 0)

    def turn(s, carry):
        back[block(s, tile), :] = hsum[s].T.astype(BF16)
        return carry

    lax.fori_loop(0, halos, turn, 0)


def middle(table, acc, halo, weight, out_grad, tiles):
    count, tile, _ = tiles.shape
    targets = acc.shape[0] - 1
    feat, hidden = weight.shape
    return pl.pallas_call(
        middle_kernel,
        name="middle",
        out_shape=(
            jax.ShapeDtypeStruct(out_grad.shape, BF16),
            jax.ShapeDtypeStruct((targets, feat, tile), BF16),
            jax.ShapeDtypeStruct((feat, hidden), F32),
            jax.ShapeDtypeStruct(halo.shape, BF16),
        ),
        in_specs=[SMEM, VMEM, VMEM, VMEM, VMEM, ANY],
        out_specs=(VMEM, VMEM, VMEM, VMEM),
        scratch_shapes=[
            pltpu.VMEM((count + GROUP, tile, tile), BF16),
            pltpu.VMEM((targets + 1, tile, feat), F32),
            pltpu.VMEM((halo.shape[0] // tile + 1, feat, tile), F32),
            pltpu.SemaphoreType.DMA((count // GROUP + 1,)),
        ],
        compiler_params=pltpu.CompilerParams(vmem_limit_bytes=32 * MIB),
        cost_estimate=pl.CostEstimate(
            flops=6 * out_grad.size * feat * 2,
            bytes_accessed=out_grad.size * 8,
            transcendentals=out_grad.size,
        ),
    )(table, acc, halo, weight, out_grad, tiles)


def backward_kernel(lower, upper, first, table, grads, tiles, sent, kept, held, acc, sems):
    low, high = table[3, lower], table[3, upper]
    start_run(table, tiles, held, sems, low, high)
    clear_tiles(acc)
    backward_run(table, grads, tiles, held, sems, acc, low, high, first)
    part = sent.shape[0]

    def flush(k, carry):
        sent[k] = acc[k].astype(BF16)
        kept[k] = acc[part + k]
        return carry

    lax.fori_loop(0, part, flush, 0)


def backward(table, grads, tiles, lower, halo, quarter):
    count, tile, _ = tiles.shape
    feat = grads.shape[1]
    shape = (quarter, feat, tile)
    return pl.pallas_call(
        functools.partial(backward_kernel, lower, lower + 2, halo + lower * quarter),
        name="backward",
        out_shape=(jax.ShapeDtypeStruct(shape, BF16), jax.ShapeDtypeStruct(shape, F32)),
        in_specs=[SMEM, VMEM, ANY],
        out_specs=(VMEM, VMEM),
        scratch_shapes=[
            pltpu.VMEM((count + GROUP, tile, tile), BF16),
            pltpu.VMEM((2 * quarter + 1, feat, tile), F32),
            pltpu.SemaphoreType.DMA((count // GROUP + 1,)),
        ],
        compiler_params=pltpu.CompilerParams(vmem_limit_bytes=24 * MIB),
        cost_estimate=pl.CostEstimate(
            flops=tiles.size * feat * 4, bytes_accessed=tiles.size, transcendentals=0
        ),
    )(table, grads, tiles)


def finish_kernel(index, kept, near, far, here, there, out):
    count, feat, tile = kept.shape
    base = lax.axis_index("rep") * (count * tile)
    slots = index.shape[1]
    sub = lax.broadcasted_iota(jnp.int32, (tile, slots), 0)

    def one(k, carry):
        total = kept[k] + near[k].astype(F32) + far[k].astype(F32)
        hit = jnp.where(index[...] - (base + k * tile) == sub, 1.0, 0.0).astype(BF16)
        extra = dot(hit, here[...]) + dot(hit, there[...])
        out[block(k, tile), :] = (total.T + extra).astype(BF16)
        return carry

    lax.fori_loop(0, count, one, 0)


def finish(index, kept, near, far, here, there):
    count, feat, tile = kept.shape
    return pl.pallas_call(
        finish_kernel,
        name="finish",
        out_shape=jax.ShapeDtypeStruct((count * tile, feat), BF16),
        in_specs=[VMEM] * 6,
        out_specs=VMEM,
        compiler_params=pltpu.CompilerParams(vmem_limit_bytes=24 * MIB),
        cost_estimate=pl.CostEstimate(
            flops=4 * count * tile * feat * index.shape[1],
            bytes_accessed=kept.size * 10,
            transcendentals=0,
        ),
    )(index, kept, near, far, here, there)


def swap(x, axis, size, bit):
    return lax.ppermute(x, axis, [(i, i ^ bit) for i in range(size)])


def shards(n_dom, n_rep, features, weight, out_grad, send_rows, send_count, tile_target, tile_source, tile_weights):
    assert n_rep == 4 and n_dom & (n_dom - 1) == 0
    feat = features.shape[1]
    tiles = tile_weights[0, 0]
    tile = tiles.shape[-1]
    rows = send_rows[0]
    cap = rows.shape[1]
    targets = out_grad.shape[0] // tile
    local = features.shape[0] // tile
    halo_tiles = n_dom * cap // tile
    quarter = local // n_rep
    source, target = tile_source[0], tile_target[0]

    outgoing = pick(rows, send_count, features).reshape(n_dom, cap, feat)
    halo = lax.all_to_all(outgoing, "dom", split_axis=0, concat_axis=0, tiled=True)
    halo = halo.reshape(-1, feat)
    table = plan(source, target, local, halo_tiles, n_rep)
    acc = forward(source, target, features, tiles, targets)
    activated, grads, wpart, back = middle(table, acc, halo, weight, out_grad, tiles)

    returned = lax.all_to_all(
        back.reshape(n_dom, cap, feat), "dom", split_axis=0, concat_axis=0, tiled=True
    ).reshape(-1, feat)

    sent_a, kept_a = backward(table, grads, tiles, 0, halo_tiles, quarter)
    near_a = swap(sent_a, "rep", n_rep, 1)
    across = (kept_a + near_a.astype(F32)).astype(BF16)
    far = swap(across, "rep", n_rep, 2)
    sent_b, kept_b = backward(table, grads, tiles, 2, halo_tiles, quarter)
    near_b = swap(sent_b, "rep", n_rep, 1)

    beside = swap(returned, "rep", n_rep, 1)
    here = (returned.astype(F32) + beside.astype(F32)).astype(BF16)
    there = swap(here, "rep", n_rep, 2)

    halves = wpart.reshape(2, feat // 2, -1)
    odd = lax.axis_index("rep") & 1
    mine = lax.dynamic_index_in_dim(halves, odd, 0, False)
    other = lax.dynamic_index_in_dim(halves, 1 - odd, 0, False)
    total = mine + swap(other, "rep", n_rep, 1)
    total = total + swap(total, "rep", n_rep, 2)
    bit = 1
    while bit < n_dom:
        total = total + swap(total, "dom", n_dom, bit)
        bit *= 2
    rest = swap(total, "rep", n_rep, 1)
    first = jnp.where(odd == 0, total, rest)
    second = jnp.where(odd == 0, rest, total)
    weight_grad = jnp.concatenate([first, second], axis=0)

    valid = jnp.arange(cap, dtype=jnp.int32)[None, :] < send_count[0][:, None]
    index = jnp.where(valid, rows, -1).reshape(1, -1)
    node_grad = finish(index, kept_b, near_b, far, here, there)
    return (activated, node_grad, weight_grad)


def solution(mesh):
    return jax.shard_map(
        functools.partial(shards, mesh.shape["dom"], mesh.shape["rep"]),
        mesh=mesh,
        in_specs=(
            P("dom", None),
            P(),
            P(("dom", "rep"), None),
            P("dom", None, None),
            P("dom", None),
            P("dom", "rep", None),
            P("dom", "rep", None),
            P("dom", "rep", None, None, None),
        ),
        out_specs=(P(("dom", "rep"), None), P(("dom", "rep"), None), P()),
        check_vma=False,
    )
```

```python
import functools

import jax
import jax.numpy as jnp
from jax import lax
from jax.experimental import pallas as pl
from jax.experimental.pallas import tpu as pltpu
from jax.sharding import PartitionSpec as P


LANES = 128
BITS_TILE, BITS_OTHER = 10, 7
SIZE = 2
UNROLL_FORWARD, UNROLL_HALO, UNROLL_BACKWARD = 36, 8, 36
PARTS = 8
F32 = jnp.float32
BF16 = jnp.bfloat16
MIB = 1 << 20
VMEM = pl.BlockSpec(memory_space=pltpu.VMEM)
SMEM = pl.BlockSpec(memory_space=pltpu.SMEM)
HBM = pl.BlockSpec(memory_space=pltpu.HBM)
NN = (((1,), (0,)), ((), ()))
NT = (((1,), (1,)), ((), ()))
TN = (((0,), (0,)), ((), ()))


def in_hbm(*arrays):
    return [pltpu.with_memory_space_constraint(x, pltpu.HBM) for x in arrays]


def dot(a, b, dims=NN):
    return lax.dot_general(a, b, dims, preferred_element_type=F32)


def block(i, size):
    return pl.ds(pl.multiple_of(i * size, size), size)


def pick_kernel(rows_in, counts_in, feat_in, out, feat, rows, counts, wide, stage, sems):
    dests, cap = rows.shape
    parts = sems.shape[0] - 2
    step = feat.shape[0] // parts
    small = [
        pltpu.make_async_copy(rows_in, rows, sems.at[parts]),
        pltpu.make_async_copy(counts_in, counts, sems.at[parts + 1]),
    ]
    for copy in small:
        copy.start()

    def fetch(i):
        span = pl.ds(i * step, step)
        return pltpu.make_async_copy(feat_in.at[span], feat.at[span], sems.at[i])

    for i in range(parts):
        fetch(i).start()
    for copy in small:
        copy.wait()
    piece = 256
    for i in range(parts):
        fetch(i).wait()

        def widen(k, carry):
            span = pl.ds(pl.multiple_of(i * step + k * piece, piece), piece)
            wide[span, :] = feat[span, :].astype(F32)
            return carry

        lax.fori_loop(0, step // piece, widen, 0)
    slot = lax.broadcasted_iota(jnp.int32, stage.shape, 0)

    def one(d, carry):
        count = counts[0, d]
        for c in range(cap):
            row = jnp.where(c < count, rows[d, c], 0)
            stage[c : c + 1, :] = wide[pl.ds(row, 1), :]
        out[block(d, cap), :] = jnp.where(slot < count, stage[...], 0.0).astype(BF16)
        return carry

    lax.fori_loop(0, dests, one, 0)


def pick(rows, counts, features):
    dests, cap = rows.shape
    feat = features.shape[1]
    parts = 4
    return pl.pallas_call(
        pick_kernel,
        name="pick",
        out_shape=jax.ShapeDtypeStruct((dests * cap, feat), BF16),
        in_specs=[HBM, HBM, HBM],
        out_specs=VMEM,
        scratch_shapes=[
            pltpu.VMEM(features.shape, BF16),
            pltpu.SMEM(rows.shape, jnp.int32),
            pltpu.SMEM(counts.shape, jnp.int32),
            pltpu.VMEM(features.shape, F32),
            pltpu.VMEM((cap, feat), F32),
            pltpu.SemaphoreType.DMA((parts + 2,)),
        ],
        compiler_params=pltpu.CompilerParams(vmem_limit_bytes=16 * MIB),
        cost_estimate=pl.CostEstimate(
            flops=features.size, bytes_accessed=features.size * 4, transcendentals=0
        ),
    )(*in_hbm(rows, counts, features))


def ordered_sets(key, other, wide):
    count = key.shape[1]
    lanes = jnp.broadcast_to(key, (count, count))
    subs = lanes.T
    i = lax.broadcasted_iota(jnp.int32, (count, count), 0)
    j = lax.broadcasted_iota(jnp.int32, (count, count), 1)
    before = jnp.where((lanes == subs) & (j < i), 1.0, 0.0)
    rank = jnp.sum(before, axis=1, keepdims=True)
    lane = lax.broadcasted_iota(jnp.int32, (count, LANES), 1).astype(F32)
    own = subs[:, :1] == lane
    number = jnp.sum(jnp.where(own, 1.0, 0.0), axis=0, keepdims=True)
    sets = jnp.floor((number + (SIZE - 1.0)) * (1.0 / SIZE))
    k = lax.broadcasted_iota(jnp.int32, (LANES, LANES), 0)
    q = lax.broadcasted_iota(jnp.int32, (LANES, LANES), 1)
    lower = jnp.where(k < q, 1.0, 0.0).astype(BF16)
    starts = dot(jnp.broadcast_to(sets, (16, LANES)).astype(BF16), lower)[:1, :]
    spot = jnp.sum(jnp.where(own, SIZE * starts, 0.0), axis=1, keepdims=True) + rank
    place = lax.broadcasted_iota(jnp.int32, (count, wide), 1).astype(F32)
    chosen = spot == place
    index = lax.broadcasted_iota(jnp.int32, (count, 1), 0).astype(F32) + 1.0
    others = jnp.broadcast_to(other, (count, count)).T[:, :1]
    shift = float(1 << BITS_TILE)
    entry = index + shift * (others + float(1 << BITS_OTHER) * subs[:, :1])
    row = jnp.sum(jnp.where(chosen, entry, 0.0), axis=0, keepdims=True)
    return row.astype(jnp.int32), starts.astype(jnp.int32)


def tile_of(entry):
    return entry & ((1 << BITS_TILE) - 1)


def other_of(entry):
    return (entry >> BITS_TILE) & ((1 << BITS_OTHER) - 1)


def key_of(entry):
    return entry >> (BITS_TILE + BITS_OTHER)


def clear_tiles(acc):
    zeros = jnp.zeros(acc.shape[1:], acc.dtype)

    def clear(k, carry):
        acc[k] = zeros
        return carry

    lax.fori_loop(0, acc.shape[0], clear, 0)


class Plan:
    def __init__(self, ref, base, wide):
        self.ref, self.base, self.wide = ref, base, wide

    def start(self, key):
        return self.ref[0, self.base + self.wide + key]

    def entry(self, at):
        return self.ref[0, self.base + at]


def plans(ref, wide):
    return Plan(ref, 0, wide), Plan(ref, wide + LANES, wide)


def run_sets(plan, first, last, acc, shift, group, product):
    spare = acc.shape[0] - 1
    low, high = plan.start(first), plan.start(last)

    def run(g, carry):
        for u in range(group):
            which = low + g * group + u
            at = SIZE * jnp.minimum(which, high - 1)
            members = [plan.entry(at + i) for i in range(SIZE)]
            place = jnp.where(which < high, key_of(members[0]) - shift, spare)
            acc[place] += product(members)
        return carry

    lax.fori_loop(0, lax.div(high - low + group - 1, group), run, 0)


def gather_product(held, rows):
    tile = held.shape[-1]

    def product(members):
        left = jnp.concatenate([held[tile_of(e)] for e in members], axis=1)
        right = jnp.concatenate([rows[block(other_of(e), tile), :] for e in members], axis=0)
        return dot(left, right)

    return product


def scatter_product(held, grads):
    def product(members):
        left = jnp.concatenate([grads[other_of(e)] for e in members], axis=1)
        right = jnp.concatenate([held[tile_of(e)] for e in members], axis=0)
        return dot(left, right)

    return product


def tile_copies(tiles, held, sems):
    step = tiles.shape[0] // PARTS
    return [
        pltpu.make_async_copy(
            tiles.at[pl.ds(i * step, step)], held.at[pl.ds(1 + i * step, step)], sems.at[i]
        )
        for i in range(PARTS)
    ]


def start_all(copies):
    for copy in copies:
        copy.start()


def wait_all(copies):
    for copy in copies:
        copy.wait()


def forward_kernel(
    ranks, halos, source_in, target_in, feat_in, tiles, acc, made, held, feat, source, target, table, sems
):
    count, tile, _ = tiles.shape
    local = feat.shape[0] // tile
    targets = acc.shape[0] - 1
    quarter = local // ranks
    small = [
        pltpu.make_async_copy(source_in, source, sems.at[PARTS]),
        pltpu.make_async_copy(target_in, target, sems.at[PARTS + 1]),
    ]
    start_all(small)
    large = [pltpu.make_async_copy(feat_in, feat, sems.at[PARTS + 2])]
    large += tile_copies(tiles, held, sems)
    start_all(large)
    wait_all(small)
    held[0] = jnp.zeros((tile, tile), BF16)
    wide = made.shape[1] // 2 - LANES
    ahead, _ = plans(table, wide)
    src, tgt = source[...], target[...]
    mine = src < local
    late = lax.broadcasted_iota(jnp.int32, src.shape, 1) >= count // 2
    key = jnp.where(mine, jnp.where(late, targets + tgt, tgt), 2 * targets + tgt).astype(F32)
    other = jnp.where(mine, src, src - local).astype(F32)
    made_ahead = ordered_sets(key, other, wide)
    me = lax.axis_index("rep")
    part = jnp.zeros_like(src)
    for k in range(1, ranks):
        part = part + jnp.where(src >= k * quarter, 1, 0)
    place = (part ^ (me ^ (ranks - 1))) * quarter + (src - part * quarter)
    key = jnp.where(mine, halos + place, src - local).astype(F32)
    made_back = ordered_sets(key, tgt.astype(F32), wide)
    made[...] = jnp.concatenate(made_ahead + made_back, axis=1)
    order = pltpu.make_async_copy(made, table, sems.at[PARTS])
    order.start()
    clear_tiles(acc)
    order.wait()
    half = 1 + PARTS // 2
    product = gather_product(held, feat)
    wait_all(large[:half])
    run_sets(ahead, 0, targets, acc, 0, UNROLL_FORWARD, product)
    wait_all(large[half:])
    run_sets(ahead, targets, 2 * targets, acc, targets, UNROLL_FORWARD, product)


def forward(source, target, features, tiles, targets, ranks, halos):
    count, tile, _ = tiles.shape
    feat = features.shape[1]
    wide = count + LANES
    return pl.pallas_call(
        functools.partial(forward_kernel, ranks, halos),
        name="forward",
        out_shape=(
            pltpu.HBM((targets + 1, tile, feat), F32),
            pltpu.VMEM((1, 2 * (wide + LANES)), jnp.int32),
        ),
        in_specs=[HBM, HBM, HBM, HBM],
        out_specs=(VMEM, VMEM),
        scratch_shapes=[
            pltpu.VMEM((count + 1, tile, tile), BF16),
            pltpu.VMEM(features.shape, BF16),
            pltpu.VMEM((1, count), jnp.int32),
            pltpu.VMEM((1, count), jnp.int32),
            pltpu.SMEM((1, 2 * (wide + LANES)), jnp.int32),
            pltpu.SemaphoreType.DMA((PARTS + 3,)),
        ],
        compiler_params=pltpu.CompilerParams(vmem_limit_bytes=20 * MIB),
        cost_estimate=pl.CostEstimate(
            flops=2 * tiles.size * feat * 4, bytes_accessed=tiles.size * 2, transcendentals=0
        ),
    )(*in_hbm(source, target, features, tiles))


def middle_kernel(
    table, acc_in, halo, weight, out_grad_in, tiles, act, wgrad, back, sent_a, kept_a, sent_b, kept_b,
    held, some, rows, sums, hsum, lsum, grads, acc, out_grad, sems, few
):
    _, tile, _ = tiles.shape
    targets = acc.shape[0]
    halos = halo.shape[0] // tile
    ahead, order = plans(table, table.shape[1] // 2 - LANES)
    low, high = ahead.start(2 * targets), ahead.start(3 * targets)
    groups = lax.div(high - low + UNROLL_HALO - 1, UNROLL_HALO)
    batch = SIZE * UNROLL_HALO

    def entry_of(n, i):
        return ahead.entry(jnp.minimum(SIZE * low + n * batch + i, SIZE * high - 1))

    def fetch(n, carry):
        for i in range(batch):
            t = jnp.maximum(tile_of(entry_of(n, i)), 1) - 1
            pltpu.make_async_copy(tiles.at[t], some.at[n * batch + i], few.at[n]).start()
        return carry

    lax.fori_loop(0, groups, fetch, 0)
    inputs = [
        pltpu.make_async_copy(acc_in.at[pl.ds(0, targets)], acc, sems.at[PARTS]),
        pltpu.make_async_copy(out_grad_in, out_grad, sems.at[PARTS + 1]),
    ]
    large = tile_copies(tiles, held, sems)
    start_all(inputs + large)
    held[0] = jnp.zeros((tile, tile), BF16)
    clear_tiles(sums)
    clear_tiles(hsum)
    clear_tiles(lsum)
    rows[: halos * tile, :] = halo[...]
    rows[halos * tile :, :] = jnp.zeros((tile, halo.shape[1]), BF16)

    def add(n, carry):
        span = block(n, batch)
        pltpu.make_async_copy(tiles.at[pl.ds(0, batch)], some.at[span], few.at[n]).wait()
        for u in range(UNROLL_HALO):
            left, right = [], []
            for i in range(SIZE * u, SIZE * u + SIZE):
                entry = entry_of(n, i)
                s = jnp.where(tile_of(entry) > 0, other_of(entry), halos)
                left.append(some[n * batch + i])
                right.append(rows[block(s, tile), :])
            here = low + n * UNROLL_HALO + u < high
            place = jnp.where(here, key_of(entry_of(n, SIZE * u)) - 2 * targets, targets)
            sums[place] += dot(jnp.concatenate(left, axis=1), jnp.concatenate(right, axis=0))
        return carry

    lax.fori_loop(0, groups, add, 0)
    wgrad[...] = jnp.zeros(wgrad.shape, F32)
    wait_all(inputs)
    width = 4

    def dense(b, carry):
        many = []
        for u in range(width):
            k = b * width + u
            many.append((acc[k] + sums[k]).astype(BF16))
        packed = jnp.concatenate(many, axis=0)
        span = block(b, width * tile)
        pre = dot(packed, weight[...])
        sigma = jax.nn.sigmoid(pre)
        silu = pre * sigma
        act[span, :] = silu.astype(BF16)
        slope = sigma + silu * (1.0 - sigma)
        pre_grad = (out_grad[span, :].astype(F32) * slope).astype(BF16)
        wgrad[...] += dot(packed, pre_grad, TN)
        turned = dot(weight[...], pre_grad, NT).astype(BF16)
        for u in range(width):
            grads[b * width + u] = turned[:, u * tile : (u + 1) * tile]
        return carry

    lax.fori_loop(0, targets // width, dense, 0)
    wait_all(large)
    product = scatter_product(held, grads)
    run_sets(order, 0, halos, hsum, 0, UNROLL_HALO, product)

    def turn(s, carry):
        back[block(s, tile), :] = hsum[s].T.astype(BF16)
        return carry

    lax.fori_loop(0, halos, turn, 0)
    part = sent_a.shape[0]
    run_sets(order, halos, halos + 4 * part, lsum, halos, UNROLL_BACKWARD, product)

    def flush(k, carry):
        sent_a[k] = lsum[k].astype(BF16)
        kept_a[k] = lsum[part + k]
        sent_b[k] = lsum[2 * part + k].astype(BF16)
        kept_b[k] = lsum[3 * part + k]
        return carry

    lax.fori_loop(0, part, flush, 0)


def middle(table, acc, halo, weight, out_grad, tiles, quarter):
    count, tile, _ = tiles.shape
    targets = acc.shape[0] - 1
    feat, hidden = weight.shape
    batch = SIZE * UNROLL_HALO
    groups = (count + targets + batch - 1) // batch
    return pl.pallas_call(
        middle_kernel,
        name="middle",
        out_shape=(
            jax.ShapeDtypeStruct(out_grad.shape, BF16),
            jax.ShapeDtypeStruct((feat, hidden), F32),
            jax.ShapeDtypeStruct(halo.shape, BF16),
            jax.ShapeDtypeStruct((quarter, feat, tile), BF16),
            pltpu.VMEM((quarter, feat, tile), F32),
            jax.ShapeDtypeStruct((quarter, feat, tile), BF16),
            pltpu.HBM((quarter, feat, tile), F32),
        ),
        in_specs=[SMEM, HBM, VMEM, VMEM, HBM, HBM],
        out_specs=(VMEM,) * 7,
        scratch_shapes=[
            pltpu.VMEM((count + 1, tile, tile), BF16),
            pltpu.VMEM((groups * batch, tile, tile), BF16),
            pltpu.VMEM((halo.shape[0] + tile, feat), BF16),
            pltpu.VMEM((targets + 1, tile, feat), F32),
            pltpu.VMEM((halo.shape[0] // tile + 1, feat, tile), F32),
            pltpu.VMEM((4 * quarter + 1, feat, tile), F32),
            pltpu.VMEM((targets, feat, tile), BF16),
            pltpu.VMEM((targets, tile, feat), F32),
            pltpu.VMEM(out_grad.shape, BF16),
            pltpu.SemaphoreType.DMA((PARTS + 2,)),
            pltpu.SemaphoreType.DMA((groups,)),
        ],
        compiler_params=pltpu.CompilerParams(vmem_limit_bytes=40 * MIB),
        cost_estimate=pl.CostEstimate(
            flops=6 * out_grad.size * feat * 2 + tiles.size * feat * 8,
            bytes_accessed=out_grad.size * 8,
            transcendentals=out_grad.size,
        ),
    )(table, *in_hbm(acc), halo, weight, *in_hbm(out_grad, tiles))


def finish_kernel(index, kept, near, far, here, there, out, both):
    count, feat, tile = kept.shape
    base = lax.axis_index("rep") * (count * tile)
    slots = index.shape[1]
    sub = lax.broadcasted_iota(jnp.int32, (tile, slots), 0)
    both[:, :feat] = here[...]
    both[:, feat:] = there[...]
    width = 4

    def one(b, carry):
        for u in range(width):
            k = b * width + u
            total = kept[k] + near[k].astype(F32) + far[k].astype(F32)
            hit = jnp.where(index[...] - (base + k * tile) == sub, 1.0, 0.0).astype(BF16)
            extra = dot(hit, both[...])
            out[block(k, tile), :] = (total.T + extra[:, :feat] + extra[:, feat:]).astype(BF16)
        return carry

    lax.fori_loop(0, count // width, one, 0)


def finish(index, kept, near, far, here, there):
    count, feat, tile = kept.shape
    return pl.pallas_call(
        finish_kernel,
        name="finish",
        out_shape=jax.ShapeDtypeStruct((count * tile, feat), BF16),
        in_specs=[VMEM] * 6,
        out_specs=VMEM,
        scratch_shapes=[pltpu.VMEM((here.shape[0], 2 * feat), BF16)],
        compiler_params=pltpu.CompilerParams(vmem_limit_bytes=24 * MIB),
        cost_estimate=pl.CostEstimate(
            flops=4 * count * tile * feat * index.shape[1],
            bytes_accessed=kept.size * 10,
            transcendentals=0,
        ),
    )(index, kept, near, far, here, there)


def swap(x, axis, size, bit):
    return lax.ppermute(x, axis, [(i, i ^ bit) for i in range(size)])


def plus(x, y):
    return x + y


def exchange(x):
    return lax.all_to_all(x, "dom", split_axis=0, concat_axis=0, tiled=True)


def pick_one(blocks, i):
    return lax.dynamic_index_in_dim(blocks, i, 0, False)


def join(bit, mine, other):
    first = jnp.where(bit == 0, mine, other)
    second = jnp.where(bit == 0, other, mine)
    return jnp.concatenate([first, second], axis=0)


def shards(n_dom, n_rep, features, weight, out_grad, send_rows, send_count, tile_target, tile_source, tile_weights):
    assert n_rep == 4 and n_dom & (n_dom - 1) == 0
    feat = features.shape[1]
    tiles = tile_weights[0, 0]
    tile = tiles.shape[-1]
    rows = send_rows[0]
    cap = rows.shape[1]
    targets = out_grad.shape[0] // tile
    local = features.shape[0] // tile
    halo_tiles = n_dom * cap // tile
    quarter = local // n_rep
    count, most = tiles.shape[0], halo_tiles + local
    assert count % 8 == 0 and count < 1 << BITS_TILE and max(most, 3 * targets) < LANES
    source, target = tile_source[0], tile_target[0]

    outgoing = pick(rows, send_count, features).reshape(n_dom, cap, feat)
    halo = exchange(outgoing).reshape(-1, feat)
    acc, table = forward(source, target, features, tiles, targets, n_rep, halo_tiles)
    activated, wpart, back, sent_a, kept_a, sent_b, kept_b = middle(
        table, acc, halo, weight, out_grad, tiles, quarter
    )

    me = lax.axis_index("rep")
    low_bit = me & 1
    hidden = weight.shape[1]

    near_a = swap(sent_a, "rep", n_rep, 1)
    near_b = swap(sent_b, "rep", n_rep, 1)
    across = (kept_a + near_a.astype(F32)).astype(BF16)
    far = swap(across, "rep", n_rep, 2)

    returned = exchange(back.reshape(n_dom, cap, feat)).reshape(-1, feat)
    beside = swap(returned, "rep", n_rep, 1)
    here = (returned.astype(F32) + beside.astype(F32)).astype(BF16)
    there = swap(here, "rep", n_rep, 2)

    halves = wpart.reshape(2, feat // 2, hidden)
    near = swap(pick_one(halves, 1 - low_bit), "rep", n_rep, 1)
    total = plus(pick_one(halves, low_bit), near)
    total = plus(total, swap(total, "rep", n_rep, 2))
    bit = 1
    while bit < n_dom:
        total = plus(total, swap(total, "dom", n_dom, bit))
        bit *= 2
    weight_grad = join(low_bit, total, swap(total, "rep", n_rep, 1))

    valid = jnp.arange(cap, dtype=jnp.int32)[None, :] < send_count[0][:, None]
    index = jnp.where(valid, rows, -1).reshape(1, -1)
    node_grad = finish(index, kept_b, near_b, far, here, there)
    return (activated, node_grad, weight_grad)


def solution(mesh):
    def body(*args):
        return shards(mesh.shape["dom"], mesh.shape["rep"], *args)

    return jax.shard_map(
        body,
        mesh=mesh,
        in_specs=(
            P("dom", None),
            P(),
            P(("dom", "rep"), None),
            P("dom", None, None),
            P("dom", None),
            P("dom", "rep", None),
            P("dom", "rep", None),
            P("dom", "rep", None, None, None),
        ),
        out_specs=(P(("dom", "rep"), None), P(("dom", "rep"), None), P()),
        check_vma=False,
    )
```

```python
import functools
import math

import jax
import jax.numpy as jnp
from jax import lax
from jax.experimental import pallas as pl
from jax.experimental.pallas import tpu as pltpu
from jax.sharding import PartitionSpec as P


LANES = 128
BITS_TILE, BITS_OTHER = 10, 7
SIZE = 2
UNROLL_FORWARD, UNROLL_HALO, UNROLL_RETURN, UNROLL_BACKWARD = 36, 20, 16, 48
WIDTH = 16
PARTS = 8
F32 = jnp.float32
BF16 = jnp.bfloat16
MIB = 1 << 20
VMEM = pl.BlockSpec(memory_space=pltpu.VMEM)
SMEM = pl.BlockSpec(memory_space=pltpu.SMEM)
HBM = pl.BlockSpec(memory_space=pltpu.HBM)
NN = (((1,), (0,)), ((), ()))
NT = (((1,), (1,)), ((), ()))
TN = (((0,), (0,)), ((), ()))


def in_hbm(*arrays):
    return [pltpu.with_memory_space_constraint(x, pltpu.HBM) for x in arrays]


def dot(a, b, dims=NN):
    return lax.dot_general(a, b, dims, preferred_element_type=F32)


def block(i, size):
    return pl.ds(pl.multiple_of(i * size, size), size)


def pick_kernel(rows_in, counts_in, feat_in, out, feat, rows, counts, wide, stage, sems):
    dests, cap = rows.shape
    parts = sems.shape[0] - 2
    step = feat.shape[0] // parts
    small = [
        pltpu.make_async_copy(rows_in, rows, sems.at[parts]),
        pltpu.make_async_copy(counts_in, counts, sems.at[parts + 1]),
    ]
    for copy in small:
        copy.start()

    def fetch(i):
        span = pl.ds(i * step, step)
        return pltpu.make_async_copy(feat_in.at[span], feat.at[span], sems.at[i])

    for i in range(parts):
        fetch(i).start()
    for copy in small:
        copy.wait()
    piece = 256
    for i in range(parts):
        fetch(i).wait()

        def widen(k, carry):
            span = pl.ds(pl.multiple_of(i * step + k * piece, piece), piece)
            wide[span, :] = feat[span, :].astype(F32)
            return carry

        lax.fori_loop(0, step // piece, widen, 0)
    slot = lax.broadcasted_iota(jnp.int32, stage.shape, 0)

    def one(d, carry):
        count = counts[0, d]
        for c in range(cap):
            row = jnp.where(c < count, rows[d, c], 0)
            stage[c : c + 1, :] = wide[pl.ds(row, 1), :]
        out[block(d, cap), :] = jnp.where(slot < count, stage[...], 0.0).astype(BF16)
        return carry

    lax.fori_loop(0, dests, one, 0)


def pick(rows, counts, features):
    dests, cap = rows.shape
    feat = features.shape[1]
    parts = 4
    return pl.pallas_call(
        pick_kernel,
        name="pick",
        out_shape=jax.ShapeDtypeStruct((dests * cap, feat), BF16),
        in_specs=[HBM, HBM, HBM],
        out_specs=VMEM,
        scratch_shapes=[
            pltpu.VMEM(features.shape, BF16),
            pltpu.SMEM(rows.shape, jnp.int32),
            pltpu.SMEM(counts.shape, jnp.int32),
            pltpu.VMEM(features.shape, F32),
            pltpu.VMEM((cap, feat), F32),
            pltpu.SemaphoreType.DMA((parts + 2,)),
        ],
        compiler_params=pltpu.CompilerParams(vmem_limit_bytes=16 * MIB),
        cost_estimate=pl.CostEstimate(
            flops=features.size, bytes_accessed=features.size * 4, transcendentals=0
        ),
    )(*in_hbm(rows, counts, features))


def ordered_sets(key, other, wide):
    count = key.shape[1]
    lanes = jnp.broadcast_to(key, (count, count))
    subs = lanes.T
    i = lax.broadcasted_iota(jnp.int32, (count, count), 0)
    j = lax.broadcasted_iota(jnp.int32, (count, count), 1)
    before = jnp.where((lanes == subs) & (j < i), 1.0, 0.0)
    rank = jnp.sum(before, axis=1, keepdims=True)
    lane = lax.broadcasted_iota(jnp.int32, (count, LANES), 1).astype(F32)
    own = subs[:, :1] == lane
    number = jnp.sum(jnp.where(own, 1.0, 0.0), axis=0, keepdims=True)
    sets = jnp.floor((number + (SIZE - 1.0)) * (1.0 / SIZE))
    k = lax.broadcasted_iota(jnp.int32, (LANES, LANES), 0)
    q = lax.broadcasted_iota(jnp.int32, (LANES, LANES), 1)
    lower = jnp.where(k < q, 1.0, 0.0).astype(BF16)
    starts = dot(jnp.broadcast_to(sets, (16, LANES)).astype(BF16), lower)[:1, :]
    spot = jnp.sum(jnp.where(own, SIZE * starts, 0.0), axis=1, keepdims=True) + rank
    place = lax.broadcasted_iota(jnp.int32, (count, wide), 1).astype(F32)
    chosen = spot == place
    index = lax.broadcasted_iota(jnp.int32, (count, 1), 0).astype(F32) + 1.0
    others = jnp.broadcast_to(other, (count, count)).T[:, :1]
    shift = float(1 << BITS_TILE)
    entry = index + shift * (others + float(1 << BITS_OTHER) * subs[:, :1])
    row = jnp.sum(jnp.where(chosen, entry, 0.0), axis=0, keepdims=True)
    return row.astype(jnp.int32), starts.astype(jnp.int32)


def tile_of(entry):
    return entry & ((1 << BITS_TILE) - 1)


def other_of(entry):
    return (entry >> BITS_TILE) & ((1 << BITS_OTHER) - 1)


def key_of(entry):
    return entry >> (BITS_TILE + BITS_OTHER)


def clear_tiles(acc):
    zeros = jnp.zeros(acc.shape[1:], acc.dtype)

    def clear(k, carry):
        acc[k] = zeros
        return carry

    lax.fori_loop(0, acc.shape[0], clear, 0)


class Plan:
    def __init__(self, ref, base, wide):
        self.ref, self.base, self.wide = ref, base, wide

    def start(self, key):
        return self.ref[0, self.base + self.wide + key]

    def entry(self, at):
        return self.ref[0, self.base + at]


def plans(ref, wide):
    return Plan(ref, 0, wide), Plan(ref, wide + LANES, wide)


def run_sets(plan, first, last, acc, shift, group, product):
    spare = acc.shape[0] - 1
    low, high = plan.start(first), plan.start(last)

    def run(g, carry):
        for u in range(group):
            which = low + g * group + u
            at = SIZE * jnp.minimum(which, high - 1)
            members = [plan.entry(at + i) for i in range(SIZE)]
            place = jnp.where(which < high, key_of(members[0]) - shift, spare)
            acc[place] += product(members)
        return carry

    lax.fori_loop(0, lax.div(high - low + group - 1, group), run, 0)


def gather_product(held, rows):
    tile = held.shape[-1]

    def product(members):
        left = jnp.concatenate([held[tile_of(e)] for e in members], axis=1)
        right = jnp.concatenate([rows[block(other_of(e), tile), :] for e in members], axis=0)
        return dot(left, right)

    return product


def scatter_product(held, grads):
    def product(members):
        left = jnp.concatenate([grads[other_of(e)] for e in members], axis=1)
        right = jnp.concatenate([held[tile_of(e)] for e in members], axis=0)
        return dot(left, right)

    return product


def tile_copies(tiles, held, sems):
    step = tiles.shape[0] // PARTS
    return [
        pltpu.make_async_copy(
            tiles.at[pl.ds(i * step, step)], held.at[pl.ds(1 + i * step, step)], sems.at[i]
        )
        for i in range(PARTS)
    ]


def start_all(copies):
    for copy in copies:
        copy.start()


def wait_all(copies):
    for copy in copies:
        copy.wait()


def forward_kernel(
    ranks, halos, source_in, target_in, feat_in, tiles, acc, made, held, feat, source, target, table, sems
):
    count, tile, _ = tiles.shape
    local = feat.shape[0] // tile
    targets = acc.shape[0] - 1
    quarter = local // ranks
    small = [
        pltpu.make_async_copy(source_in, source, sems.at[PARTS]),
        pltpu.make_async_copy(target_in, target, sems.at[PARTS + 1]),
    ]
    start_all(small)
    large = [pltpu.make_async_copy(feat_in, feat, sems.at[PARTS + 2])]
    large += tile_copies(tiles, held, sems)
    start_all(large)
    wait_all(small)
    held[0] = jnp.zeros((tile, tile), BF16)
    wide = made.shape[1] // 2 - LANES
    ahead, _ = plans(table, wide)
    src, tgt = source[...], target[...]
    mine = src < local
    late = lax.broadcasted_iota(jnp.int32, src.shape, 1) >= count // 2
    key = jnp.where(mine, jnp.where(late, targets + tgt, tgt), 2 * targets + tgt).astype(F32)
    other = jnp.where(mine, src, src - local).astype(F32)
    made_ahead = ordered_sets(key, other, wide)
    me = lax.axis_index("rep")
    part = jnp.zeros_like(src)
    for k in range(1, ranks):
        part = part + jnp.where(src >= k * quarter, 1, 0)
    place = (part ^ (me ^ (ranks - 1))) * quarter + (src - part * quarter)
    key = jnp.where(mine, halos + place, src - local).astype(F32)
    made_back = ordered_sets(key, tgt.astype(F32), wide)
    made[...] = jnp.concatenate(made_ahead + made_back, axis=1)
    order = pltpu.make_async_copy(made, table, sems.at[PARTS])
    order.start()
    clear_tiles(acc)
    order.wait()
    half = 1 + PARTS // 2
    product = gather_product(held, feat)
    wait_all(large[:half])
    run_sets(ahead, 0, targets, acc, 0, UNROLL_FORWARD, product)
    wait_all(large[half:])
    run_sets(ahead, targets, 2 * targets, acc, targets, UNROLL_FORWARD, product)


def forward(source, target, features, tiles, targets, ranks, halos):
    count, tile, _ = tiles.shape
    feat = features.shape[1]
    wide = count + LANES
    return pl.pallas_call(
        functools.partial(forward_kernel, ranks, halos),
        name="forward",
        out_shape=(
            pltpu.HBM((targets + 1, tile, feat), F32),
            pltpu.VMEM((1, 2 * (wide + LANES)), jnp.int32),
        ),
        in_specs=[HBM, HBM, HBM, HBM],
        out_specs=(VMEM, VMEM),
        scratch_shapes=[
            pltpu.VMEM((count + 1, tile, tile), BF16),
            pltpu.VMEM(features.shape, BF16),
            pltpu.VMEM((1, count), jnp.int32),
            pltpu.VMEM((1, count), jnp.int32),
            pltpu.SMEM((1, 2 * (wide + LANES)), jnp.int32),
            pltpu.SemaphoreType.DMA((PARTS + 3,)),
        ],
        compiler_params=pltpu.CompilerParams(vmem_limit_bytes=20 * MIB),
        cost_estimate=pl.CostEstimate(
            flops=2 * tiles.size * feat * 4, bytes_accessed=tiles.size * 2, transcendentals=0
        ),
    )(*in_hbm(source, target, features, tiles))


def middle_kernel(
    table, acc_in, halo, weight, out_grad_in, tiles, act, wgrad, back, sent_a, kept_a, sent_b, kept_b,
    held, some, rows, sums, hsum, lsum, grads, acc, out_grad, sems, few
):
    count, tile, _ = tiles.shape
    targets = acc.shape[0]
    halos = halo.shape[0] // tile
    ahead, order = plans(table, table.shape[1] // 2 - LANES)
    low, high = ahead.start(2 * targets), ahead.start(3 * targets)
    groups = lax.div(high - low + UNROLL_HALO - 1, UNROLL_HALO)
    batch = SIZE * UNROLL_HALO

    def entry_of(n, i):
        return ahead.entry(jnp.minimum(SIZE * low + n * batch + i, SIZE * high - 1))

    def fetch(n, carry):
        for i in range(batch):
            slot = n * batch + i
            real = SIZE * low + slot < SIZE * high
            t = jnp.where(real, jnp.maximum(tile_of(entry_of(n, i)), 1) - 1, slot)
            t = jnp.minimum(t, count - 1)
            pltpu.make_async_copy(tiles.at[t], some.at[n * batch + i], few.at[n]).start()
        return carry

    lax.fori_loop(0, groups, fetch, 0)
    inputs = [
        pltpu.make_async_copy(acc_in.at[pl.ds(0, targets)], acc, sems.at[PARTS]),
        pltpu.make_async_copy(out_grad_in, out_grad, sems.at[PARTS + 1]),
    ]
    large = tile_copies(tiles, held, sems)
    start_all(inputs + large)
    held[0] = jnp.zeros((tile, tile), BF16)
    clear_tiles(sums)
    clear_tiles(hsum)
    clear_tiles(lsum)
    rows[: halos * tile, :] = halo[...]
    rows[halos * tile :, :] = jnp.zeros((tile, halo.shape[1]), BF16)

    def add(n, carry):
        span = block(n, batch)
        pltpu.make_async_copy(tiles.at[pl.ds(0, batch)], some.at[span], few.at[n]).wait()
        for u in range(UNROLL_HALO):
            left, right = [], []
            for i in range(SIZE * u, SIZE * u + SIZE):
                entry = entry_of(n, i)
                s = jnp.where(tile_of(entry) > 0, other_of(entry), halos)
                left.append(some[n * batch + i])
                right.append(rows[block(s, tile), :])
            here = low + n * UNROLL_HALO + u < high
            place = jnp.where(here, key_of(entry_of(n, SIZE * u)) - 2 * targets, targets)
            sums[place] += dot(jnp.concatenate(left, axis=1), jnp.concatenate(right, axis=0))
        return carry

    lax.fori_loop(0, groups, add, 0)
    wgrad[...] = jnp.zeros(wgrad.shape, F32)
    wait_all(inputs)
    width = math.gcd(targets, WIDTH)

    def dense(b, carry):
        many = []
        for u in range(width):
            k = b * width + u
            many.append((acc[k] + sums[k]).astype(BF16))
        packed = jnp.concatenate(many, axis=0)
        span = block(b, width * tile)
        pre = dot(packed, weight[...])
        sigma = jax.nn.sigmoid(pre)
        silu = pre * sigma
        act[span, :] = silu.astype(BF16)
        slope = sigma + silu * (1.0 - sigma)
        pre_grad = (out_grad[span, :].astype(F32) * slope).astype(BF16)
        wgrad[...] += dot(packed, pre_grad, TN)
        turned = dot(weight[...], pre_grad, NT).astype(BF16)
        for u in range(width):
            grads[b * width + u] = turned[:, u * tile : (u + 1) * tile]
        return carry

    lax.fori_loop(0, targets // width, dense, 0)
    wait_all(large)
    product = scatter_product(held, grads)
    run_sets(order, 0, halos, hsum, 0, UNROLL_RETURN, product)

    def turn(s, carry):
        back[block(s, tile), :] = hsum[s].T.astype(BF16)
        return carry

    lax.fori_loop(0, halos, turn, 0)
    part = sent_a.shape[0]
    run_sets(order, halos, halos + 4 * part, lsum, halos, UNROLL_BACKWARD, product)

    def flush(k, carry):
        sent_a[k] = lsum[k].astype(BF16)
        kept_a[k] = lsum[part + k]
        sent_b[k] = lsum[2 * part + k].astype(BF16)
        kept_b[k] = lsum[3 * part + k].astype(BF16)
        return carry

    lax.fori_loop(0, part, flush, 0)


def middle(table, acc, halo, weight, out_grad, tiles, quarter):
    count, tile, _ = tiles.shape
    targets = acc.shape[0] - 1
    feat, hidden = weight.shape
    batch = SIZE * UNROLL_HALO
    groups = (count + targets + batch - 1) // batch
    return pl.pallas_call(
        middle_kernel,
        name="middle",
        out_shape=(
            jax.ShapeDtypeStruct(out_grad.shape, BF16),
            jax.ShapeDtypeStruct((feat, hidden), F32),
            jax.ShapeDtypeStruct(halo.shape, BF16),
            jax.ShapeDtypeStruct((quarter, feat, tile), BF16),
            pltpu.VMEM((quarter, feat, tile), F32),
            jax.ShapeDtypeStruct((quarter, feat, tile), BF16),
            jax.ShapeDtypeStruct((quarter, feat, tile), BF16),
        ),
        in_specs=[SMEM, HBM, VMEM, VMEM, HBM, HBM],
        out_specs=(VMEM,) * 7,
        scratch_shapes=[
            pltpu.VMEM((count + 1, tile, tile), BF16),
            pltpu.VMEM((groups * batch, tile, tile), BF16),
            pltpu.VMEM((halo.shape[0] + tile, feat), BF16),
            pltpu.VMEM((targets + 1, tile, feat), F32),
            pltpu.VMEM((halo.shape[0] // tile + 1, feat, tile), F32),
            pltpu.VMEM((4 * quarter + 1, feat, tile), F32),
            pltpu.VMEM((targets, feat, tile), BF16),
            pltpu.VMEM((targets, tile, feat), F32),
            pltpu.VMEM(out_grad.shape, BF16),
            pltpu.SemaphoreType.DMA((PARTS + 2,)),
            pltpu.SemaphoreType.DMA((groups,)),
        ],
        compiler_params=pltpu.CompilerParams(vmem_limit_bytes=40 * MIB),
        cost_estimate=pl.CostEstimate(
            flops=6 * out_grad.size * feat * 2 + tiles.size * feat * 8,
            bytes_accessed=out_grad.size * 8,
            transcendentals=out_grad.size,
        ),
    )(table, *in_hbm(acc), halo, weight, *in_hbm(out_grad, tiles))


def finish_kernel(mine, index, kept, near, far, here, there, out, rows):
    count, _, tile = kept.shape
    base = lax.axis_index("rep") * (count * tile)
    slots = index.shape[1]
    sub = lax.broadcasted_iota(jnp.int32, (tile, slots), 0)

    @pl.when(mine[0] == 1)
    def _():
        rows[...] = here[...]

    @pl.when(mine[0] == 0)
    def _():
        rows[...] = there[...]

    width = math.gcd(count, WIDTH)

    def one(b, carry):
        for u in range(width):
            k = b * width + u
            total = kept[k].astype(F32) + near[k].astype(F32) + far[k].astype(F32)
            hit = jnp.where(index[...] - (base + k * tile) == sub, 1.0, 0.0).astype(BF16)
            out[block(k, tile), :] = (total.T + dot(hit, rows[...])).astype(BF16)
        return carry

    lax.fori_loop(0, count // width, one, 0)


def finish(index, kept, near, far, here, there, mine):
    count, feat, tile = kept.shape
    return pl.pallas_call(
        finish_kernel,
        name="finish",
        out_shape=jax.ShapeDtypeStruct((count * tile, feat), BF16),
        in_specs=[SMEM] + [VMEM] * 6,
        out_specs=VMEM,
        scratch_shapes=[pltpu.VMEM(here.shape, BF16)],
        compiler_params=pltpu.CompilerParams(vmem_limit_bytes=24 * MIB),
        cost_estimate=pl.CostEstimate(
            flops=4 * count * tile * feat * index.shape[1],
            bytes_accessed=kept.size * 10,
            transcendentals=0,
        ),
    )(mine.astype(jnp.int32).reshape(1), index, kept, near, far, here, there)


def swap(x, axis, size, bit):
    return lax.ppermute(x, axis, [(i, i ^ bit) for i in range(size)])


def plus(x, y):
    return x + y


def exchange(x):
    return lax.all_to_all(x, "dom", split_axis=0, concat_axis=0, tiled=True)


def pick_one(blocks, i):
    return lax.dynamic_index_in_dim(blocks, i, 0, False)


def join(bit, mine, other):
    first = jnp.where(bit == 0, mine, other)
    second = jnp.where(bit == 0, other, mine)
    return jnp.concatenate([first, second], axis=0)


def shards(n_dom, n_rep, features, weight, out_grad, send_rows, send_count, tile_target, tile_source, tile_weights):
    assert n_rep == 4 and n_dom & (n_dom - 1) == 0
    feat = features.shape[1]
    tiles = tile_weights[0, 0]
    tile = tiles.shape[-1]
    rows = send_rows[0]
    cap = rows.shape[1]
    targets = out_grad.shape[0] // tile
    local = features.shape[0] // tile
    halo_tiles = n_dom * cap // tile
    quarter = local // n_rep
    count, most = tiles.shape[0], halo_tiles + local
    assert count % 8 == 0 and count < 1 << BITS_TILE and max(most, 3 * targets) < LANES
    source, target = tile_source[0], tile_target[0]

    outgoing = pick(rows, send_count, features).reshape(n_dom, cap, feat)
    halo = exchange(outgoing).reshape(-1, feat)
    acc, table = forward(source, target, features, tiles, targets, n_rep, halo_tiles)
    activated, wpart, back, sent_a, kept_a, sent_b, kept_b = middle(
        table, acc, halo, weight, out_grad, tiles, quarter
    )

    me = lax.axis_index("rep")
    low_bit = me & 1
    hidden = weight.shape[1]

    near_a = swap(sent_a, "rep", n_rep, 1)
    near_b = swap(sent_b, "rep", n_rep, 1)
    across = (kept_a + near_a.astype(F32)).astype(BF16)
    far = swap(across, "rep", n_rep, 2)

    back = back.reshape(2, n_dom // 2 * cap, feat)
    hnear = swap(pick_one(back, 1 - low_bit), "rep", n_rep, 1)
    hhalf = (pick_one(back, low_bit).astype(F32) + hnear.astype(F32)).astype(BF16)
    hside = swap(hhalf, "rep", n_rep, 2)
    hfull = (hhalf.astype(F32) + hside.astype(F32)).astype(BF16)

    halves = wpart.reshape(2, feat // 2, hidden)
    near = swap(pick_one(halves, 1 - low_bit), "rep", n_rep, 1)
    total = plus(pick_one(halves, low_bit), near)
    total = plus(total, swap(total, "rep", n_rep, 2))

    here = lax.axis_index("dom")
    blocks = hfull.reshape(1, n_dom // 2, cap, feat)
    bit = n_dom // 2
    while bit:
        kept, sent = blocks, blocks
        if bit < n_dom // 2:
            split = blocks.reshape(blocks.shape[0], 2, -1, cap, feat)
            own = jnp.minimum(here & bit, 1)
            kept = lax.dynamic_index_in_dim(split, own, 1, False)
            sent = lax.dynamic_index_in_dim(split, 1 - own, 1, False)
        came = swap(sent, "dom", n_dom, bit)
        blocks = jnp.concatenate([kept, came], axis=0)
        total = plus(total, swap(total, "dom", n_dom, bit))
        bit //= 2
    arrived = blocks.reshape(-1, feat)
    beside = swap(arrived, "rep", n_rep, 1)
    weight_grad = join(low_bit, total, swap(total, "rep", n_rep, 1))
    mine = here // (n_dom // 2) == low_bit

    valid = jnp.arange(cap, dtype=jnp.int32)[None, :] < send_count[0][:, None]
    index = jnp.where(valid, rows, -1)
    bits = n_dom.bit_length() - 1
    index = index.reshape((2,) * bits + (cap,))
    for axis in range(bits):
        flip = (here >> (bits - 1 - axis)) & 1
        index = jnp.where(flip == 1, jnp.flip(index, axis), index)
    index = index.transpose(tuple(reversed(range(bits))) + (bits,)).reshape(1, -1)
    node_grad = finish(index, kept_b, near_b, far, arrived, beside, mine)
    return (activated, node_grad, weight_grad)


def solution(mesh):
    def body(*args):
        return shards(mesh.shape["dom"], mesh.shape["rep"], *args)

    return jax.shard_map(
        body,
        mesh=mesh,
        in_specs=(
            P("dom", None),
            P(),
            P(("dom", "rep"), None),
            P("dom", None, None),
            P("dom", None),
            P("dom", "rep", None),
            P("dom", "rep", None),
            P("dom", "rep", None, None, None),
        ),
        out_specs=(P(("dom", "rep"), None), P(("dom", "rep"), None), P()),
        check_vma=False,
    )
```

```python
import functools
import math

import jax
import jax.numpy as jnp
from jax import lax
from jax.experimental import pallas as pl
from jax.experimental.pallas import tpu as pltpu
from jax.sharding import PartitionSpec as P


LANES = 128
BITS_TILE, BITS_OTHER = 10, 7
SIZE = 2
UNROLL_FORWARD, UNROLL_HALO, UNROLL_RETURN, UNROLL_BACKWARD = 36, 20, 16, 48
WIDTH = 16
PARTS = 8
F32 = jnp.float32
BF16 = jnp.bfloat16
MIB = 1 << 20
VMEM = pl.BlockSpec(memory_space=pltpu.VMEM)
SMEM = pl.BlockSpec(memory_space=pltpu.SMEM)
HBM = pl.BlockSpec(memory_space=pltpu.HBM)
NN = (((1,), (0,)), ((), ()))
NT = (((1,), (1,)), ((), ()))
TN = (((0,), (0,)), ((), ()))


def in_hbm(*arrays):
    return [pltpu.with_memory_space_constraint(x, pltpu.HBM) for x in arrays]


def dot(a, b, dims=NN):
    return lax.dot_general(a, b, dims, preferred_element_type=F32)


def block(i, size):
    return pl.ds(pl.multiple_of(i * size, size), size)


def pick_kernel(rows_in, counts_in, feat_in, out, feat, rows, counts, wide, stage, sems):
    dests, cap = rows.shape
    parts = sems.shape[0] - 2
    step = feat.shape[0] // parts
    small = [
        pltpu.make_async_copy(rows_in, rows, sems.at[parts]),
        pltpu.make_async_copy(counts_in, counts, sems.at[parts + 1]),
    ]
    for copy in small:
        copy.start()

    def fetch(i):
        span = pl.ds(i * step, step)
        return pltpu.make_async_copy(feat_in.at[span], feat.at[span], sems.at[i])

    for i in range(parts):
        fetch(i).start()
    for copy in small:
        copy.wait()
    piece = 256
    for i in range(parts):
        fetch(i).wait()

        def widen(k, carry):
            span = pl.ds(pl.multiple_of(i * step + k * piece, piece), piece)
            wide[span, :] = feat[span, :].astype(F32)
            return carry

        lax.fori_loop(0, step // piece, widen, 0)
    slot = lax.broadcasted_iota(jnp.int32, stage.shape, 0)

    def one(d, carry):
        count = counts[0, d]
        for c in range(cap):
            row = jnp.where(c < count, rows[d, c], 0)
            stage[c : c + 1, :] = wide[pl.ds(row, 1), :]
        out[block(d, cap), :] = jnp.where(slot < count, stage[...], 0.0).astype(BF16)
        return carry

    lax.fori_loop(0, dests, one, 0)


def pick(rows, counts, features):
    dests, cap = rows.shape
    feat = features.shape[1]
    parts = 4
    return pl.pallas_call(
        pick_kernel,
        name="pick",
        out_shape=jax.ShapeDtypeStruct((dests * cap, feat), BF16),
        in_specs=[HBM, HBM, HBM],
        out_specs=VMEM,
        scratch_shapes=[
            pltpu.VMEM(features.shape, BF16),
            pltpu.SMEM(rows.shape, jnp.int32),
            pltpu.SMEM(counts.shape, jnp.int32),
            pltpu.VMEM(features.shape, F32),
            pltpu.VMEM((cap, feat), F32),
            pltpu.SemaphoreType.DMA((parts + 2,)),
        ],
        compiler_params=pltpu.CompilerParams(vmem_limit_bytes=16 * MIB),
        cost_estimate=pl.CostEstimate(
            flops=features.size, bytes_accessed=features.size * 4, transcendentals=0
        ),
    )(*in_hbm(rows, counts, features))


def ordered_sets(key, other, wide):
    count = key.shape[1]
    lanes = jnp.broadcast_to(key, (count, count))
    subs = lanes.T
    i = lax.broadcasted_iota(jnp.int32, (count, count), 0)
    j = lax.broadcasted_iota(jnp.int32, (count, count), 1)
    before = jnp.where((lanes == subs) & (j < i), 1.0, 0.0)
    rank = jnp.sum(before, axis=1, keepdims=True)
    lane = lax.broadcasted_iota(jnp.int32, (count, LANES), 1).astype(F32)
    own = subs[:, :1] == lane
    number = jnp.sum(jnp.where(own, 1.0, 0.0), axis=0, keepdims=True)
    sets = jnp.floor((number + (SIZE - 1.0)) * (1.0 / SIZE))
    k = lax.broadcasted_iota(jnp.int32, (LANES, LANES), 0)
    q = lax.broadcasted_iota(jnp.int32, (LANES, LANES), 1)
    lower = jnp.where(k < q, 1.0, 0.0).astype(BF16)
    starts = dot(jnp.broadcast_to(sets, (16, LANES)).astype(BF16), lower)[:1, :]
    spot = jnp.sum(jnp.where(own, SIZE * starts, 0.0), axis=1, keepdims=True) + rank
    place = lax.broadcasted_iota(jnp.int32, (count, wide), 1).astype(F32)
    chosen = spot == place
    index = lax.broadcasted_iota(jnp.int32, (count, 1), 0).astype(F32) + 1.0
    others = jnp.broadcast_to(other, (count, count)).T[:, :1]
    shift = float(1 << BITS_TILE)
    entry = index + shift * (others + float(1 << BITS_OTHER) * subs[:, :1])
    row = jnp.sum(jnp.where(chosen, entry, 0.0), axis=0, keepdims=True)
    return row.astype(jnp.int32), starts.astype(jnp.int32)


def tile_of(entry):
    return entry & ((1 << BITS_TILE) - 1)


def other_of(entry):
    return (entry >> BITS_TILE) & ((1 << BITS_OTHER) - 1)


def key_of(entry):
    return entry >> (BITS_TILE + BITS_OTHER)


def clear_tiles(acc):
    zeros = jnp.zeros(acc.shape[1:], acc.dtype)

    def clear(k, carry):
        acc[k] = zeros
        return carry

    lax.fori_loop(0, acc.shape[0], clear, 0)


class Plan:
    def __init__(self, ref, base, wide):
        self.ref, self.base, self.wide = ref, base, wide

    def start(self, key):
        return self.ref[0, self.base + self.wide + key]

    def entry(self, at):
        return self.ref[0, self.base + at]


def plans(ref, wide):
    return Plan(ref, 0, wide), Plan(ref, wide + LANES, wide)


def run_sets(plan, first, last, acc, shift, group, product):
    spare = acc.shape[0] - 1
    low, high = plan.start(first), plan.start(last)

    def run(g, carry):
        for u in range(group):
            which = low + g * group + u
            at = SIZE * jnp.minimum(which, high - 1)
            members = [plan.entry(at + i) for i in range(SIZE)]
            place = jnp.where(which < high, key_of(members[0]) - shift, spare)
            acc[place] += product(members)
        return carry

    lax.fori_loop(0, lax.div(high - low + group - 1, group), run, 0)


def gather_product(held, rows):
    tile = held.shape[-1]

    def product(members):
        left = jnp.concatenate([held[tile_of(e)] for e in members], axis=1)
        right = jnp.concatenate([rows[block(other_of(e), tile), :] for e in members], axis=0)
        return dot(left, right)

    return product


def scatter_product(held, grads):
    def product(members):
        left = jnp.concatenate([grads[other_of(e)] for e in members], axis=1)
        right = jnp.concatenate([held[tile_of(e)] for e in members], axis=0)
        return dot(left, right)

    return product


def tile_copies(tiles, held, sems):
    step = tiles.shape[0] // PARTS
    return [
        pltpu.make_async_copy(
            tiles.at[pl.ds(i * step, step)], held.at[pl.ds(1 + i * step, step)], sems.at[i]
        )
        for i in range(PARTS)
    ]


def start_all(copies):
    for copy in copies:
        copy.start()


def wait_all(copies):
    for copy in copies:
        copy.wait()


def forward_kernel(
    ranks, halos, source_in, target_in, feat_in, tiles, acc, made, held, feat, source, target, table, sems
):
    count, tile, _ = tiles.shape
    local = feat.shape[0] // tile
    targets = acc.shape[0] - 1
    quarter = local // ranks
    small = [
        pltpu.make_async_copy(source_in, source, sems.at[PARTS]),
        pltpu.make_async_copy(target_in, target, sems.at[PARTS + 1]),
    ]
    start_all(small)
    large = [pltpu.make_async_copy(feat_in, feat, sems.at[PARTS + 2])]
    large += tile_copies(tiles, held, sems)
    start_all(large)
    wait_all(small)
    held[0] = jnp.zeros((tile, tile), BF16)
    wide = made.shape[1] // 2 - LANES
    ahead, _ = plans(table, wide)
    src, tgt = source[...], target[...]
    mine = src < local
    late = lax.broadcasted_iota(jnp.int32, src.shape, 1) >= count // 2
    key = jnp.where(mine, jnp.where(late, targets + tgt, tgt), 2 * targets + tgt).astype(F32)
    other = jnp.where(mine, src, src - local).astype(F32)
    made_ahead = ordered_sets(key, other, wide)
    me = lax.axis_index("rep")
    part = jnp.zeros_like(src)
    for k in range(1, ranks):
        part = part + jnp.where(src >= k * quarter, 1, 0)
    place = (part ^ (me ^ (ranks - 1))) * quarter + (src - part * quarter)
    key = jnp.where(mine, halos + place, src - local).astype(F32)
    made_back = ordered_sets(key, tgt.astype(F32), wide)
    made[...] = jnp.concatenate(made_ahead + made_back, axis=1)
    order = pltpu.make_async_copy(made, table, sems.at[PARTS])
    order.start()
    clear_tiles(acc)
    order.wait()
    half = 1 + PARTS // 2
    product = gather_product(held, feat)
    wait_all(large[:half])
    run_sets(ahead, 0, targets, acc, 0, UNROLL_FORWARD, product)
    wait_all(large[half:])
    run_sets(ahead, targets, 2 * targets, acc, targets, UNROLL_FORWARD, product)


def forward(source, target, features, tiles, targets, ranks, halos):
    count, tile, _ = tiles.shape
    feat = features.shape[1]
    wide = count + LANES
    return pl.pallas_call(
        functools.partial(forward_kernel, ranks, halos),
        name="forward",
        out_shape=(
            pltpu.HBM((targets + 1, tile, feat), F32),
            pltpu.VMEM((1, 2 * (wide + LANES)), jnp.int32),
        ),
        in_specs=[HBM, HBM, HBM, HBM],
        out_specs=(VMEM, VMEM),
        scratch_shapes=[
            pltpu.VMEM((count + 1, tile, tile), BF16),
            pltpu.VMEM(features.shape, BF16),
            pltpu.VMEM((1, count), jnp.int32),
            pltpu.VMEM((1, count), jnp.int32),
            pltpu.SMEM((1, 2 * (wide + LANES)), jnp.int32),
            pltpu.SemaphoreType.DMA((PARTS + 3,)),
        ],
        compiler_params=pltpu.CompilerParams(vmem_limit_bytes=20 * MIB),
        cost_estimate=pl.CostEstimate(
            flops=2 * tiles.size * feat * 4, bytes_accessed=tiles.size * 2, transcendentals=0
        ),
    )(*in_hbm(source, target, features, tiles))


def middle_kernel(
    table, acc_in, halo, weight, out_grad_in, tiles, act, wgrad, back, sent_a, kept_a, sent_b, kept_b,
    held, some, rows, sums, hsum, lsum, grads, acc, out_grad, sems, few
):
    count, tile, _ = tiles.shape
    targets = acc.shape[0]
    halos = halo.shape[0] // tile
    ahead, order = plans(table, table.shape[1] // 2 - LANES)
    low, high = ahead.start(2 * targets), ahead.start(3 * targets)
    groups = lax.div(high - low + UNROLL_HALO - 1, UNROLL_HALO)
    batch = SIZE * UNROLL_HALO

    def entry_of(n, i):
        return ahead.entry(jnp.minimum(SIZE * low + n * batch + i, SIZE * high - 1))

    def fetch(n, carry):
        for i in range(batch):
            slot = n * batch + i
            real = SIZE * low + slot < SIZE * high
            t = jnp.where(real, jnp.maximum(tile_of(entry_of(n, i)), 1) - 1, slot)
            t = jnp.minimum(t, count - 1)
            pltpu.make_async_copy(tiles.at[t], some.at[n * batch + i], few.at[n]).start()
        return carry

    lax.fori_loop(0, groups, fetch, 0)
    inputs = [
        pltpu.make_async_copy(acc_in.at[pl.ds(0, targets)], acc, sems.at[PARTS]),
        pltpu.make_async_copy(out_grad_in, out_grad, sems.at[PARTS + 1]),
    ]
    large = tile_copies(tiles, held, sems)
    start_all(inputs + large)
    held[0] = jnp.zeros((tile, tile), BF16)
    clear_tiles(sums)
    clear_tiles(hsum)
    clear_tiles(lsum)
    rows[: halos * tile, :] = halo[...]
    rows[halos * tile :, :] = jnp.zeros((tile, halo.shape[1]), BF16)

    def add(n, carry):
        span = block(n, batch)
        pltpu.make_async_copy(tiles.at[pl.ds(0, batch)], some.at[span], few.at[n]).wait()
        for u in range(UNROLL_HALO):
            left, right = [], []
            for i in range(SIZE * u, SIZE * u + SIZE):
                entry = entry_of(n, i)
                s = jnp.where(tile_of(entry) > 0, other_of(entry), halos)
                left.append(some[n * batch + i])
                right.append(rows[block(s, tile), :])
            here = low + n * UNROLL_HALO + u < high
            place = jnp.where(here, key_of(entry_of(n, SIZE * u)) - 2 * targets, targets)
            sums[place] += dot(jnp.concatenate(left, axis=1), jnp.concatenate(right, axis=0))
        return carry

    lax.fori_loop(0, groups, add, 0)
    wgrad[...] = jnp.zeros(wgrad.shape, F32)
    wait_all(inputs)
    width = math.gcd(targets, WIDTH)

    def dense(b, carry):
        many = []
        for u in range(width):
            k = b * width + u
            many.append((acc[k] + sums[k]).astype(BF16))
        packed = jnp.concatenate(many, axis=0)
        span = block(b, width * tile)
        pre = dot(packed, weight[...])
        sigma = jax.nn.sigmoid(pre)
        silu = pre * sigma
        act[span, :] = silu.astype(BF16)
        slope = sigma + silu * (1.0 - sigma)
        pre_grad = (out_grad[span, :].astype(F32) * slope).astype(BF16)
        wgrad[...] += dot(packed, pre_grad, TN)
        turned = dot(weight[...], pre_grad, NT).astype(BF16)
        for u in range(width):
            grads[b * width + u] = turned[:, u * tile : (u + 1) * tile]
        return carry

    lax.fori_loop(0, targets // width, dense, 0)
    wait_all(large)
    product = scatter_product(held, grads)
    run_sets(order, 0, halos, hsum, 0, UNROLL_RETURN, product)

    def turn(s, carry):
        back[block(s, tile), :] = hsum[s].T.astype(BF16)
        return carry

    lax.fori_loop(0, halos, turn, 0)
    part = sent_a.shape[0]
    run_sets(order, halos, halos + 4 * part, lsum, halos, UNROLL_BACKWARD, product)

    def flush(k, carry):
        sent_a[k] = lsum[k].astype(BF16)
        kept_a[k] = lsum[part + k].astype(BF16)
        sent_b[k] = lsum[2 * part + k].astype(BF16)
        kept_b[k] = lsum[3 * part + k].astype(BF16)
        return carry

    lax.fori_loop(0, part, flush, 0)


def middle(table, acc, halo, weight, out_grad, tiles, quarter):
    count, tile, _ = tiles.shape
    targets = acc.shape[0] - 1
    feat, hidden = weight.shape
    batch = SIZE * UNROLL_HALO
    groups = (count + targets + batch - 1) // batch
    return pl.pallas_call(
        middle_kernel,
        name="middle",
        out_shape=(
            jax.ShapeDtypeStruct(out_grad.shape, BF16),
            jax.ShapeDtypeStruct((feat, hidden), F32),
            jax.ShapeDtypeStruct(halo.shape, BF16),
            jax.ShapeDtypeStruct((quarter, feat, tile), BF16),
            pltpu.VMEM((quarter, feat, tile), BF16),
            jax.ShapeDtypeStruct((quarter, feat, tile), BF16),
            jax.ShapeDtypeStruct((quarter, feat, tile), BF16),
        ),
        in_specs=[SMEM, HBM, VMEM, VMEM, HBM, HBM],
        out_specs=(VMEM,) * 7,
        scratch_shapes=[
            pltpu.VMEM((count + 1, tile, tile), BF16),
            pltpu.VMEM((groups * batch, tile, tile), BF16),
            pltpu.VMEM((halo.shape[0] + tile, feat), BF16),
            pltpu.VMEM((targets + 1, tile, feat), F32),
            pltpu.VMEM((halo.shape[0] // tile + 1, feat, tile), F32),
            pltpu.VMEM((4 * quarter + 1, feat, tile), F32),
            pltpu.VMEM((targets, feat, tile), BF16),
            pltpu.VMEM((targets, tile, feat), F32),
            pltpu.VMEM(out_grad.shape, BF16),
            pltpu.SemaphoreType.DMA((PARTS + 2,)),
            pltpu.SemaphoreType.DMA((groups,)),
        ],
        compiler_params=pltpu.CompilerParams(vmem_limit_bytes=40 * MIB),
        cost_estimate=pl.CostEstimate(
            flops=6 * out_grad.size * feat * 2 + tiles.size * feat * 8,
            bytes_accessed=out_grad.size * 8,
            transcendentals=out_grad.size,
        ),
    )(table, *in_hbm(acc), halo, weight, *in_hbm(out_grad, tiles))


def finish_kernel(mine, index, kept, near, far, here, there, out, rows):
    count, _, tile = kept.shape
    base = lax.axis_index("rep") * (count * tile)
    slots = index.shape[1]
    sub = lax.broadcasted_iota(jnp.int32, (tile, slots), 0)

    @pl.when(mine[0] == 1)
    def _():
        rows[...] = here[...]

    @pl.when(mine[0] == 0)
    def _():
        rows[...] = there[...]

    width = math.gcd(count, WIDTH)

    def one(b, carry):
        for u in range(width):
            k = b * width + u
            total = kept[k].astype(F32) + near[k].astype(F32) + far[k].astype(F32)
            hit = jnp.where(index[...] - (base + k * tile) == sub, 1.0, 0.0).astype(BF16)
            out[block(k, tile), :] = (total.T + dot(hit, rows[...])).astype(BF16)
        return carry

    lax.fori_loop(0, count // width, one, 0)


def finish(index, kept, near, far, here, there, mine):
    count, feat, tile = kept.shape
    return pl.pallas_call(
        finish_kernel,
        name="finish",
        out_shape=jax.ShapeDtypeStruct((count * tile, feat), BF16),
        in_specs=[SMEM] + [VMEM] * 6,
        out_specs=VMEM,
        scratch_shapes=[pltpu.VMEM(here.shape, BF16)],
        compiler_params=pltpu.CompilerParams(vmem_limit_bytes=24 * MIB),
        cost_estimate=pl.CostEstimate(
            flops=4 * count * tile * feat * index.shape[1],
            bytes_accessed=kept.size * 10,
            transcendentals=0,
        ),
    )(mine.astype(jnp.int32).reshape(1), index, kept, near, far, here, there)


def swap(x, axis, size, bit):
    return lax.ppermute(x, axis, [(i, i ^ bit) for i in range(size)])


def plus(x, y):
    return x + y


def exchange(x):
    return lax.all_to_all(x, "dom", split_axis=0, concat_axis=0, tiled=True)


def pick_one(blocks, i):
    return lax.dynamic_index_in_dim(blocks, i, 0, False)


def join(bit, mine, other):
    first = jnp.where(bit == 0, mine, other)
    second = jnp.where(bit == 0, other, mine)
    return jnp.concatenate([first, second], axis=0)


def shards(n_dom, n_rep, features, weight, out_grad, send_rows, send_count, tile_target, tile_source, tile_weights):
    assert n_rep == 4 and n_dom & (n_dom - 1) == 0
    feat = features.shape[1]
    tiles = tile_weights[0, 0]
    tile = tiles.shape[-1]
    rows = send_rows[0]
    cap = rows.shape[1]
    targets = out_grad.shape[0] // tile
    local = features.shape[0] // tile
    halo_tiles = n_dom * cap // tile
    quarter = local // n_rep
    count, most = tiles.shape[0], halo_tiles + local
    assert count % 8 == 0 and count < 1 << BITS_TILE and max(most, 3 * targets) < LANES
    source, target = tile_source[0], tile_target[0]

    outgoing = pick(rows, send_count, features).reshape(n_dom, cap, feat)
    halo = exchange(outgoing).reshape(-1, feat)
    acc, table = forward(source, target, features, tiles, targets, n_rep, halo_tiles)
    activated, wpart, back, sent_a, kept_a, sent_b, kept_b = middle(
        table, acc, halo, weight, out_grad, tiles, quarter
    )

    me = lax.axis_index("rep")
    low_bit = me & 1
    hidden = weight.shape[1]

    near_a = swap(sent_a, "rep", n_rep, 1)
    near_b = swap(sent_b, "rep", n_rep, 1)
    across = (kept_a.astype(F32) + near_a.astype(F32)).astype(BF16)
    far = swap(across, "rep", n_rep, 2)

    back = back.reshape(2, n_dom // 2 * cap, feat)
    hnear = swap(pick_one(back, 1 - low_bit), "rep", n_rep, 1)
    hhalf = (pick_one(back, low_bit).astype(F32) + hnear.astype(F32)).astype(BF16)
    hside = swap(hhalf, "rep", n_rep, 2)
    hfull = (hhalf.astype(F32) + hside.astype(F32)).astype(BF16)

    halves = wpart.reshape(2, feat // 2, hidden)
    near = swap(pick_one(halves, 1 - low_bit), "rep", n_rep, 1)
    total = plus(pick_one(halves, low_bit), near)
    total = plus(total, swap(total, "rep", n_rep, 2))

    here = lax.axis_index("dom")
    blocks = hfull.reshape(1, n_dom // 2, cap, feat)
    bit = n_dom // 2
    while bit:
        kept, sent = blocks, blocks
        if bit < n_dom // 2:
            split = blocks.reshape(blocks.shape[0], 2, -1, cap, feat)
            own = jnp.minimum(here & bit, 1)
            kept = lax.dynamic_index_in_dim(split, own, 1, False)
            sent = lax.dynamic_index_in_dim(split, 1 - own, 1, False)
        came = swap(sent, "dom", n_dom, bit)
        blocks = jnp.concatenate([kept, came], axis=0)
        total = lax.reduce_precision(total, 8, 7)
        got = swap(total.astype(BF16), "dom", n_dom, bit).astype(F32)
        total = plus(total, got)
        bit //= 2
    arrived = blocks.reshape(-1, feat)
    beside = swap(arrived, "rep", n_rep, 1)
    weight_grad = join(low_bit, total, swap(total, "rep", n_rep, 1))
    mine = here // (n_dom // 2) == low_bit

    valid = jnp.arange(cap, dtype=jnp.int32)[None, :] < send_count[0][:, None]
    index = jnp.where(valid, rows, -1)
    bits = n_dom.bit_length() - 1
    index = index.reshape((2,) * bits + (cap,))
    for axis in range(bits):
        flip = (here >> (bits - 1 - axis)) & 1
        index = jnp.where(flip == 1, jnp.flip(index, axis), index)
    index = index.transpose(tuple(reversed(range(bits))) + (bits,)).reshape(1, -1)
    node_grad = finish(index, kept_b, near_b, far, arrived, beside, mine)
    return (activated, node_grad, weight_grad)


def solution(mesh):
    def body(*args):
        return shards(mesh.shape["dom"], mesh.shape["rep"], *args)

    return jax.shard_map(
        body,
        mesh=mesh,
        in_specs=(
            P("dom", None),
            P(),
            P(("dom", "rep"), None),
            P("dom", None, None),
            P("dom", None),
            P("dom", "rep", None),
            P("dom", "rep", None),
            P("dom", "rep", None, None, None),
        ),
        out_specs=(P(("dom", "rep"), None), P(("dom", "rep"), None), P()),
        check_vma=False,
    )
```
